32 devices in a mesh: row: 8 (over z, core), col: 4 (over y, x).
Axes of the slice: x: 2, y: 2, z: 4, core: 2. Of those that a mesh axis runs over, the one named last changes fastest.
Arguments:
- tiles: bfloat16 [4096, 128, 128], P(('row', 'col')), may hold values from -48 to 48
- tile_rows: int32 [4096], P(('row', 'col')), may hold values from 0 to 1023, as said below
- tile_cols: int32 [4096], P(('row', 'col')), may hold values from 0 to 1023, as said below
- tile_count: int32 [32], P(('row', 'col')), may hold values from 32 to 128, as said below
- degree: int32 [1024, 128], P(('row', 'col')), may hold values from 32 to 96
- labels: int32 [1024, 128], P(('row', 'col')), may hold values from 0 to 63
Outputs:
- scores: float32 [1024, 16, 128], P(('row', 'col'))
The draws below stay inside these ranges and needn't reach their ends.
Inputs may be any that keep to these rules, and one draw needn't show every extreme that they name: tile_rows of the slots of device (r, c) lie in node-row blocks r * 128 to (r + 1) * 128 - 1. tile_cols of the slots of device (r, c) lie in node blocks (s * 4 + c) * 32 + o for some s below 8 and o below 32. `tile_count`: some device has all its slots live.
All inputs are finite; a program needn't handle non-finite values.
Results may differ from the reference program's by a relative error of at most 0.0039.
Values may be sent and summed in bfloat16 or wider, within the bound.
No kernel may reach another device: no remote copies, remote signals or barrier semaphores. Data moves between devices by JAX's collectives and lax.ppermute only.
A program may use at most 64 MiB of HBM per device.

```python
import jax
import jax.numpy as jnp
from jax import lax

QC = 16
BLOCK = 128
ITERS = 2
BLK_DEV = 32
TILES_DEV = 128
NB = 1024
RBLK = 128
NTILES = 4096
N_ROW = 8
N_COL = 4
DEVICES = 32


def draw_tile_rows(key, part):
    slot = jnp.arange(NTILES, dtype=jnp.int32)
    device = slot // TILES_DEV
    row_group = device // N_COL
    offset = jax.random.randint(jax.random.fold_in(key, 11), (NTILES,), 0, RBLK, dtype=jnp.int32)
    return row_group * RBLK + offset


def draw_tile_cols(key, part):
    slot = jnp.arange(NTILES, dtype=jnp.int32)
    device = slot // TILES_DEV
    col_group = device % N_COL
    which = jax.random.randint(jax.random.fold_in(key, 21), (NTILES,), 0, N_ROW, dtype=jnp.int32)
    offset = jax.random.randint(jax.random.fold_in(key, 22), (NTILES,), 0, BLK_DEV, dtype=jnp.int32)
    return (which * N_COL + col_group) * BLK_DEV + offset


def draw_tile_count(key, part):
    counts = jax.random.randint(jax.random.fold_in(key, 31), (DEVICES,), TILES_DEV // 4, TILES_DEV + 1, dtype=jnp.int32)
    full = jax.random.randint(jax.random.fold_in(key, 32), (), 0, DEVICES, dtype=jnp.int32)
    return jnp.where(jnp.arange(DEVICES, dtype=jnp.int32) == full, TILES_DEV, counts)


def plant(entries, rng, low, high):
    longest = entries.shape.index(max(entries.shape))
    spots = []
    for shift in (0, 1):
        where = [jax.random.randint(jax.random.fold_in(rng, axis), (), 0, length) for axis, length in enumerate(entries.shape)]
        where[longest] = (where[longest] + shift) % entries.shape[longest]
        spots.append(tuple(where))
    return entries.at[spots[0]].set(low).at[spots[1]].set(high)


def shard_levels(rng, extent, split, least, top_value):
    factor_of = 1.0
    for position, parts in split:
        heights = jax.random.uniform(jax.random.fold_in(jax.random.fold_in(rng, 6), position), (parts,), jnp.float32, least / len(split), top_value / len(split))
        factor_of = factor_of * jnp.repeat(jnp.exp(heights), extent[position] // parts).reshape((-1,) + (1,) * (len(extent) - 1 - position))
    return factor_of


def noise(rng, dims, deviation, bound, shards=(), kind=jnp.bfloat16):
    gain = shard_levels(rng, dims, shards, -0.22, 0.18) if shards else 1.0
    array = jax.random.normal(rng, dims, jnp.float32) * deviation * gain
    return jnp.minimum(jnp.maximum(array, -bound), bound).astype(kind)


def setup_inputs(seed: int = 0) -> dict:
    arg_keys = jax.random.split(jax.random.key(seed), 7)
    tiles = noise(arg_keys[0], (NTILES, BLOCK, BLOCK), 8.0, 48.0, ((0, 32),))
    tile_rows = draw_tile_rows(jax.random.fold_in(arg_keys[6], 71), 0)
    tile_cols = draw_tile_cols(jax.random.fold_in(arg_keys[6], 71), 0)
    tile_count = draw_tile_count(jax.random.fold_in(arg_keys[6], 71), 0)
    degree = plant(jax.random.randint(arg_keys[4], (NB, BLOCK), 32, 97), jax.random.fold_in(arg_keys[4], 1), 32, 96).astype(jnp.int32)
    labels = plant(jax.random.randint(arg_keys[5], (NB, BLOCK), 0, 4 * QC), jax.random.fold_in(arg_keys[5], 1), 0, (4 * QC) - 1).astype(jnp.int32)
    return dict(tiles=tiles, tile_rows=tile_rows, tile_cols=tile_cols, tile_count=tile_count, degree=degree, labels=labels)


def reference(tiles, tile_rows, tile_cols, tile_count, degree, labels):
    scale = 1.0 / jnp.sqrt(degree.astype(jnp.float32))
    qidx = jnp.arange(QC, dtype=jnp.int32)
    prior = (labels[:, None, :] == qidx[None, :, None]).astype(jnp.float32)
    live = (jnp.arange(TILES_DEV, dtype=jnp.int32)[None, :] < tile_count[:, None]).astype(jnp.float32)
    tiles_dev = tiles.reshape(DEVICES, TILES_DEV, BLOCK, BLOCK)
    rows_dev = tile_rows.reshape(DEVICES, TILES_DEV)
    cols_dev = tile_cols.reshape(DEVICES, TILES_DEV)
    field = prior
    for step in range(ITERS):
        scaled = (field * scale[:, None, :]).astype(jnp.bfloat16)

        def accumulate(total, xs):
            tile_set, row_set, col_set, live_set = xs
            picked = scaled[col_set].astype(jnp.float32)
            terms = jnp.einsum('tqj,tij->tqi', picked, tile_set.astype(jnp.float32))
            terms = terms * live_set[:, None, None]
            return (total.at[row_set].add(terms), None)
        start = jnp.zeros((NB, QC, BLOCK), jnp.float32)
        summed, unused = lax.scan(accumulate, start, (tiles_dev, rows_dev, cols_dev, live))
        field = 0.8 * scale[:, None, :] * summed + 0.2 * prior
    return field
```

```python
import functools

import jax
import jax.numpy as jnp
from jax import lax
from jax.experimental import pallas as pl
from jax.experimental.pallas import tpu as pltpu
from jax.sharding import PartitionSpec as P

QC = 16
ITERS = 2
CHUNK = 16

SMEM = pltpu.SMEM
VMEM = pltpu.VMEM


def div_mod(value, size):
    if size & (size - 1) == 0:
        return lax.shift_right_logical(value, size.bit_length() - 1), value & (size - 1)
    return lax.div(value, size), lax.rem(value, size)


def spread(seeded, nrow, ncol, blk, *refs):
    nz = nrow // 2
    rows_ref, cols_ref, count_ref, tiles_hbm = refs[:4]
    refs = refs[4:]
    if seeded:
        fields, refs = refs[:2], refs[2:]
    else:
        fields, refs = refs[: nrow], refs[nrow:]
    outs, refs = refs[:ncol], refs[ncol:]
    tiles, total, picks, tile_sem, pick_sem = refs
    nt = tiles.shape[0]
    row_pos, col_pos = lax.axis_index("row"), lax.axis_index("col")

    def tile_copy(i):
        part = pl.ds(i * CHUNK, CHUNK)
        return pltpu.make_async_copy(tiles_hbm.at[part], tiles.at[part], tile_sem.at[i])

    for i in range(nt // CHUNK):
        tile_copy(i).start()
    if not seeded:
        copies = [
            pltpu.make_async_copy(f, picks.at[pl.ds(i * blk, blk)], pick_sem.at[i])
            for i, f in enumerate(fields)
        ]
        for c in copies:
            c.start()
    total[...] = jnp.zeros_like(total)
    if seeded:
        for half, f in enumerate(fields):
            for i in range(nz):
                for kind in range(2):
                    picks[kind, pl.ds((half * nz + i) * blk, blk), :] = f[i, kind].astype(jnp.float32)
    else:
        for c in copies:
            c.wait()
    query = lax.broadcasted_iota(jnp.int32, (QC, 128), 0).astype(jnp.float32)
    count = count_ref[0]
    base = row_pos * blk * ncol

    def pick(t):
        owner, offset = div_mod(cols_ref[t], blk)
        source, _ = div_mod(owner, ncol)
        far = source ^ row_pos
        slot = (far & 1) * nz + lax.shift_right_logical(far, 1)
        place = slot * blk + offset
        if seeded:
            label = picks[0, pl.ds(place, 1), :]
            scale = picks[1, pl.ds(place, 1), :]
            return jnp.where(label == query, scale, 0.0).astype(jnp.bfloat16)
        return picks[place]

    def chunk(i, carry):
        tile_copy(i).wait()
        terms = []
        for u in range(CHUNK):
            t = i * CHUNK + u
            terms.append(
                lax.dot_general(
                    pick(t), tiles[t], (((1,), (1,)), ((), ())), preferred_element_type=jnp.float32
                )
            )
        for u in range(CHUNK):
            t = i * CHUNK + u
            row = jnp.where(t < count, rows_ref[t] - base, total.shape[0] - 1)
            total[row] += terms[u]
        return carry

    lax.fori_loop(0, nt // CHUNK, chunk, 0)
    for k in range(ncol):
        part = total[pl.ds((col_pos ^ k) * blk, blk)]
        outs[k][...] = part.astype(outs[k].dtype)


def spread_call(seeded, nrow, ncol, blk, rows, cols, count, tiles, fields):
    nt = tiles.shape[0]
    slots = nrow * blk
    shape = (blk, QC, 128)
    picks = pltpu.VMEM((2, slots, 128), jnp.float32) if seeded else pltpu.VMEM((slots, QC, 128), jnp.bfloat16)
    return pl.pallas_call(
        functools.partial(spread, seeded, nrow, ncol, blk),
        out_shape=[jax.ShapeDtypeStruct(shape, jnp.float32)]
        + [jax.ShapeDtypeStruct(shape, jnp.bfloat16)] * (ncol - 1),
        in_specs=[pl.BlockSpec(memory_space=SMEM)] * 3
        + [pl.BlockSpec(memory_space=pl.ANY)]
        + [pl.BlockSpec(memory_space=VMEM if seeded else pl.ANY)] * len(fields),
        out_specs=[pl.BlockSpec(memory_space=VMEM)] * ncol,
        scratch_shapes=[
            pltpu.VMEM(tiles.shape, tiles.dtype),
            pltpu.VMEM((blk * ncol + 1, QC, 128), jnp.float32),
            picks,
            pltpu.SemaphoreType.DMA((nt // CHUNK,)),
            pltpu.SemaphoreType.DMA((nrow,)),
        ],
        compiler_params=pltpu.CompilerParams(vmem_limit_bytes=24 << 20),
        cost_estimate=pl.CostEstimate(
            flops=2 * nt * QC * 128 * 128, bytes_accessed=tiles.size * 2 + slots * QC * 256, transcendentals=0
        ),
    )(rows, cols, count, tiles, *fields)


def local(nrow, ncol, tiles, tile_rows, tile_cols, tile_count, degree, labels):
    blk = labels.shape[0]
    nz = nrow // 2

    def from_row(x, d):
        return lax.ppermute(x, "row", [(i, i ^ d) for i in range(nrow)])

    def from_col(x, k):
        return lax.ppermute(x, "col", [(i, i ^ k) for i in range(ncol)])

    scale = 1.0 / jnp.sqrt(degree.astype(jnp.float32))
    qidx = jnp.arange(QC, dtype=jnp.int32)
    prior = (labels[:, None, :] == qidx[None, :, None]).astype(jnp.float32)
    for step in range(ITERS):
        if step == 0:
            own = jnp.stack([labels.astype(jnp.bfloat16), scale.astype(jnp.bfloat16)])
            near = jnp.stack([own] + [from_row(own, 2 * m) for m in range(1, nz)])
            fields = [near, from_row(near, 1)]
        else:
            own = (field * scale[:, None, :]).astype(jnp.bfloat16)
            near = [own] + [from_row(own, 2 * m) for m in range(1, nz)]
            fields = near + [from_row(x, 1) for x in near]
        outs = spread_call(step == 0, nrow, ncol, blk, tile_rows, tile_cols, tile_count, tiles, fields)
        summed = outs[0]
        for k in range(1, ncol):
            summed = summed + from_col(outs[k], k).astype(jnp.float32)
        field = 0.8 * scale[:, None, :] * summed + 0.2 * prior
    return field


def solution(mesh):
    nrow, ncol = mesh.shape["row"], mesh.shape["col"]
    return jax.shard_map(
        functools.partial(local, nrow, ncol),
        mesh=mesh,
        in_specs=(
            P(("row", "col"), None, None),
            P(("row", "col")),
            P(("row", "col")),
            P(("row", "col")),
            P(("row", "col"), None),
            P(("row", "col"), None),
        ),
        out_specs=P(("row", "col"), None, None),
        check_vma=False,
    )
```

```python
import functools

import jax
import jax.numpy as jnp
from jax import lax
from jax.experimental import pallas as pl
from jax.experimental.pallas import tpu as pltpu
from jax.sharding import PartitionSpec as P

QC = 16
ITERS = 2
COPY = 16
UNROLL = 64

HBM = pltpu.HBM
VMEM = pltpu.VMEM


def div(value, size):
    if size & (size - 1) == 0:
        return lax.shift_right_logical(value, size.bit_length() - 1)
    return lax.div(value, size)


def prepare(degree, labels, scale_ref, own_ref):
    scale = 1.0 / jnp.sqrt(degree[...].astype(jnp.float32))
    scale_ref[...] = scale
    own_ref[0] = labels[...].astype(jnp.float32).astype(jnp.bfloat16)
    own_ref[1] = scale.astype(jnp.bfloat16)


def spread(seeded, nrow, ncol, blk, *refs):
    nz = nrow // 2
    tables_hbm, tiles_hbm, refs = refs[:3], refs[3], refs[4:]
    nfields = 2 if seeded else nrow
    fields, refs = refs[:nfields], refs[nfields:]
    outs, refs = refs[:ncol], refs[ncol:]
    tiles, total, picks, rows, cols, counts, tile_sem, table_sem = refs
    nt = tiles.shape[0]
    row_pos, col_pos = lax.axis_index("row"), lax.axis_index("col")

    tables = [
        pltpu.make_async_copy(source, target, table_sem.at[i])
        for i, (source, target) in enumerate(zip(tables_hbm, (rows, cols, counts)))
    ]
    for c in tables:
        c.start()

    def tile_copy(i):
        part = pl.ds(i * COPY, COPY)
        return pltpu.make_async_copy(tiles_hbm.at[part], tiles.at[part], tile_sem.at[i])

    for i in range(nt // COPY):
        tile_copy(i).start()
    total[...] = jnp.zeros_like(total)
    if seeded:
        for half, f in enumerate(fields):
            for i in range(nz):
                for kind in range(2):
                    picks[kind, pl.ds((half * nz + i) * blk, blk), :] = f[i, kind].astype(jnp.float32)
    else:
        for i, f in enumerate(fields):
            picks[pl.ds(i * blk, blk)] = f[...]
    query = lax.broadcasted_iota(jnp.int32, (QC, 128), 0).astype(jnp.float32)
    for c in tables:
        c.wait()
    count = counts[0]
    base = row_pos * blk * ncol

    def pick(t):
        owner = div(cols[t], blk)
        offset = cols[t] - owner * blk
        far = div(owner, ncol) ^ row_pos
        slot = (far & 1) * nz + lax.shift_right_logical(far, 1)
        place = slot * blk + offset
        if seeded:
            label = picks[0, pl.ds(place, 1), :]
            scale = picks[1, pl.ds(place, 1), :]
            return jnp.where(label == query, scale, 0.0).astype(jnp.bfloat16)
        return picks[place]

    def step(i, carry):
        for j in range(UNROLL // COPY):
            tile_copy(i * (UNROLL // COPY) + j).wait()
        terms = []
        for u in range(0, UNROLL, 2):
            t = i * UNROLL + u
            pair = lax.dot_general(
                jnp.concatenate([pick(t), pick(t + 1)], 0),
                tiles[pl.ds(t, 2)].reshape(256, 128),
                (((1,), (1,)), ((), ())),
                preferred_element_type=jnp.float32,
            )
            terms += [pair[:QC, :128], pair[QC:, 128:]]
        for u in range(UNROLL):
            t = i * UNROLL + u
            row = jnp.where(t < count, rows[t] - base, total.shape[0] - 1)
            total[row] += terms[u]
        return carry

    lax.fori_loop(0, nt // UNROLL, step, 0)
    for k in range(ncol):
        part = total[pl.ds((col_pos ^ k) * blk, blk)]
        outs[k][...] = part.astype(outs[k].dtype)


def spread_call(seeded, nrow, ncol, blk, tables, tiles, fields):
    nt = tiles.shape[0]
    slots = nrow * blk
    shape = (blk, QC, 128)
    picks = pltpu.VMEM((2, slots, 128), jnp.float32) if seeded else pltpu.VMEM((slots, QC, 128), jnp.bfloat16)
    return pl.pallas_call(
        functools.partial(spread, seeded, nrow, ncol, blk),
        out_shape=[jax.ShapeDtypeStruct(shape, jnp.float32)]
        + [jax.ShapeDtypeStruct(shape, jnp.bfloat16)] * (ncol - 1),
        in_specs=[pl.BlockSpec(memory_space=HBM)] * 4 + [pl.BlockSpec(memory_space=VMEM)] * len(fields),
        out_specs=[pl.BlockSpec(memory_space=VMEM)] * ncol,
        scratch_shapes=[
            pltpu.VMEM(tiles.shape, tiles.dtype),
            pltpu.VMEM((blk * ncol + 1, QC, 128), jnp.float32),
            picks,
            *(pltpu.SMEM(x.shape, x.dtype) for x in tables),
            pltpu.SemaphoreType.DMA((nt // COPY,)),
            pltpu.SemaphoreType.DMA((len(tables),)),
        ],
        compiler_params=pltpu.CompilerParams(vmem_limit_bytes=24 << 20),
        cost_estimate=pl.CostEstimate(
            flops=2 * nt * QC * 128 * 128, bytes_accessed=tiles.size * 2 + slots * QC * 256, transcendentals=0
        ),
    )(*tables, tiles, *fields)


def local(nrow, ncol, tiles, tile_rows, tile_cols, tile_count, degree, labels):
    blk = labels.shape[0]
    nz = nrow // 2

    def from_row(x, d):
        return lax.ppermute(x, "row", [(i, i ^ d) for i in range(nrow)])

    def from_col(x, k):
        return lax.ppermute(x, "col", [(i, i ^ k) for i in range(ncol)])

    scale, seeds = pl.pallas_call(
        prepare,
        out_shape=[
            jax.ShapeDtypeStruct((blk, 128), jnp.float32),
            jax.ShapeDtypeStruct((2, blk, 128), jnp.bfloat16),
        ],
        in_specs=[pl.BlockSpec(memory_space=VMEM)] * 2,
        out_specs=[pl.BlockSpec(memory_space=VMEM)] * 2,
    )(degree, labels)
    qidx = jnp.arange(QC, dtype=jnp.int32)
    prior = (labels[:, None, :] == qidx[None, :, None]).astype(jnp.float32)
    for step in range(ITERS):
        if step == 0:
            near = jnp.stack([seeds] + [from_row(seeds, 2 * m) for m in range(1, nz)])
            fields = [near, from_row(near, 1)]
        else:
            own = (field * scale[:, None, :]).astype(jnp.bfloat16)
            near = [own] + [from_row(own, 2 * m) for m in range(1, nz)]
            fields = near + [from_row(x, 1) for x in near]
        outs = spread_call(step == 0, nrow, ncol, blk, (tile_rows, tile_cols, tile_count), tiles, fields)
        summed = outs[0]
        for k in range(1, ncol):
            summed = summed + from_col(outs[k], k).astype(jnp.float32)
        field = 0.8 * scale[:, None, :] * summed + 0.2 * prior
    return field


def solution(mesh):
    nrow, ncol = mesh.shape["row"], mesh.shape["col"]
    return jax.shard_map(
        functools.partial(local, nrow, ncol),
        mesh=mesh,
        in_specs=(
            P(("row", "col"), None, None),
            P(("row", "col")),
            P(("row", "col")),
            P(("row", "col")),
            P(("row", "col"), None),
            P(("row", "col"), None),
        ),
        out_specs=P(("row", "col"), None, None),
        check_vma=False,
    )
```

```python
import functools

import jax
import jax.numpy as jnp
from jax import lax
from jax.experimental import pallas as pl
from jax.experimental.pallas import tpu as pltpu
from jax.sharding import PartitionSpec as P

QC = 16
ITERS = 2
COPY = 16
UNROLL = 64

HBM = pltpu.HBM
VMEM = pltpu.VMEM


def div(value, size):
    if size & (size - 1) == 0:
        return lax.shift_right_logical(value, size.bit_length() - 1)
    return lax.div(value, size)


def spread(seeded, nrow, ncol, blk, *refs):
    nz = nrow // 2
    tables_hbm, tiles_hbm, counts, refs = refs[:2], refs[2], refs[3], refs[4:]
    fields, refs = refs[:nrow], refs[nrow:]
    outs, refs = refs[:ncol], refs[ncol:]
    tiles, total, picks, rows, cols, tile_sem, table_sem = refs
    nt = tiles.shape[0]
    row_pos, col_pos = lax.axis_index("row"), lax.axis_index("col")

    tables = [
        pltpu.make_async_copy(source, target, table_sem.at[i])
        for i, (source, target) in enumerate(zip(tables_hbm, (rows, cols)))
    ]
    for c in tables:
        c.start()

    def tile_copy(i):
        part = pl.ds(i * COPY, COPY)
        return pltpu.make_async_copy(tiles_hbm.at[part], tiles.at[part], tile_sem.at[i])

    for i in range(nt // COPY):
        tile_copy(i).start()
    total[...] = jnp.zeros_like(total)
    if seeded:
        for i, f in enumerate(fields):
            for kind in range(2):
                picks[kind, pl.ds(i * blk, blk), :] = f[kind].astype(jnp.float32)
    else:
        for i, f in enumerate(fields):
            picks[pl.ds(i * blk, blk)] = f[...]
    query = lax.broadcasted_iota(jnp.int32, (QC, 128), 0).astype(jnp.float32)
    for c in tables:
        c.wait()
    count = counts[0]
    base = row_pos * blk * ncol

    def pick(t):
        owner = div(cols[t], blk)
        offset = cols[t] - owner * blk
        far = div(owner, ncol) ^ row_pos
        slot = (far & 1) * nz + lax.shift_right_logical(far, 1)
        place = slot * blk + offset
        if seeded:
            label = picks[0, pl.ds(place, 1), :]
            scale = picks[1, pl.ds(place, 1), :]
            return jnp.where(label == query, scale, 0.0).astype(jnp.bfloat16)
        return picks[place]

    def step(i, carry):
        for j in range(UNROLL // COPY):
            tile_copy(i * (UNROLL // COPY) + j).wait()
        terms = []
        for u in range(0, UNROLL, 2):
            t = i * UNROLL + u
            pair = lax.dot_general(
                jnp.concatenate([pick(t), pick(t + 1)], 0),
                tiles[pl.ds(t, 2)].reshape(256, 128),
                (((1,), (1,)), ((), ())),
                preferred_element_type=jnp.float32,
            )
            terms += [pair[:QC, :128], pair[QC:, 128:]]
        for u in range(UNROLL):
            t = i * UNROLL + u
            row = jnp.where(t < count, rows[t] - base, total.shape[0] - 1)
            total[row] += terms[u]
        return carry

    lax.fori_loop(0, nt // UNROLL, step, 0)
    for k in range(ncol):
        part = total[pl.ds((col_pos ^ k) * blk, blk)]
        outs[k][...] = part.astype(outs[k].dtype)


def spread_call(seeded, nrow, ncol, blk, tables, tiles, fields):
    nt = tiles.shape[0]
    slots = nrow * blk
    shape = (blk, QC, 128)
    picks = pltpu.VMEM((2, slots, 128), jnp.float32) if seeded else pltpu.VMEM((slots, QC, 128), jnp.bfloat16)
    return pl.pallas_call(
        functools.partial(spread, seeded, nrow, ncol, blk),
        out_shape=[jax.ShapeDtypeStruct(shape, jnp.float32)]
        + [jax.ShapeDtypeStruct(shape, jnp.bfloat16)] * (ncol - 1),
        in_specs=[pl.BlockSpec(memory_space=HBM)] * 3 + [pl.BlockSpec(memory_space=pltpu.SMEM)] + [pl.BlockSpec(memory_space=VMEM)] * len(fields),
        out_specs=[pl.BlockSpec(memory_space=VMEM)] * ncol,
        scratch_shapes=[
            pltpu.VMEM(tiles.shape, tiles.dtype),
            pltpu.VMEM((blk * ncol + 1, QC, 128), jnp.float32),
            picks,
            *(pltpu.SMEM(x.shape, x.dtype) for x in tables[:2]),
            pltpu.SemaphoreType.DMA((nt // COPY,)),
            pltpu.SemaphoreType.DMA((2,)),
        ],
        compiler_params=pltpu.CompilerParams(vmem_limit_bytes=24 << 20),
        cost_estimate=pl.CostEstimate(
            flops=2 * nt * QC * 128 * 128, bytes_accessed=tiles.size * 2 + slots * QC * 256, transcendentals=0
        ),
    )(*(pltpu.with_memory_space_constraint(x, HBM) for x in (*tables[:2], tiles)), tables[2], *fields)


def local(nrow, ncol, tiles, tile_rows, tile_cols, tile_count, degree, labels):
    blk = labels.shape[0]
    nz = nrow // 2

    def from_row(x, d):
        return lax.ppermute(x, "row", [(i, i ^ d) for i in range(nrow)])

    def from_col(x, k):
        return lax.ppermute(x, "col", [(i, i ^ k) for i in range(ncol)])

    scale = 1.0 / jnp.sqrt(degree.astype(jnp.float32))
    seeds = jnp.stack([labels.astype(jnp.bfloat16), scale.astype(jnp.bfloat16)])
    qidx = jnp.arange(QC, dtype=jnp.int32)
    prior = (labels[:, None, :] == qidx[None, :, None]).astype(jnp.float32)
    for step in range(ITERS):
        if step == 0:
            own = seeds
        else:
            own = (field * scale[:, None, :]).astype(jnp.bfloat16)
        near = [own] + [from_row(own, 2 * m) for m in range(1, nz)]
        fields = near + [from_row(x, 1) for x in near]
        outs = spread_call(step == 0, nrow, ncol, blk, (tile_rows, tile_cols, tile_count), tiles, fields)
        summed = outs[0]
        for k in range(1, ncol):
            summed = summed + from_col(outs[k], k).astype(jnp.float32)
        field = 0.8 * scale[:, None, :] * summed + 0.2 * prior
    return field


def solution(mesh):
    nrow, ncol = mesh.shape["row"], mesh.shape["col"]
    return jax.shard_map(
        functools.partial(local, nrow, ncol),
        mesh=mesh,
        in_specs=(
            P(("row", "col"), None, None),
            P(("row", "col")),
            P(("row", "col")),
            P(("row", "col")),
            P(("row", "col"), None),
            P(("row", "col"), None),
        ),
        out_specs=P(("row", "col"), None, None),
        check_vma=False,
    )
```

```python
import functools

import jax
import jax.numpy as jnp
from jax import lax
from jax.experimental import pallas as pl
from jax.experimental.pallas import tpu as pltpu
from jax.sharding import PartitionSpec as P

QC = 16
ITERS = 2
COPIES = 8
UNROLL = 64

HBM = pltpu.HBM
VMEM = pltpu.VMEM
SMEM = pltpu.SMEM


def div(value, size):
    if size & (size - 1) == 0:
        return lax.shift_right_logical(value, jnp.full_like(value, size.bit_length() - 1))
    return lax.div(value, jnp.full_like(value, size))


def fetch(nrow, ncol, blk, tiles_hbm, rows_hbm, cols_hbm, count, tiles, table, rows, cols, sem):
    nt = tiles.shape[0]
    part = nt // COPIES

    def copy(i):
        some = pl.ds(i * part, part)
        return pltpu.make_async_copy(tiles_hbm.at[some], tiles.at[some], sem.at[i])

    tables = [
        pltpu.make_async_copy(source, target, sem.at[COPIES + i])
        for i, (source, target) in enumerate(((rows_hbm, rows), (cols_hbm, cols)))
    ]
    for c in tables:
        c.start()
    for i in range(COPIES):
        copy(i).start()
    for c in tables:
        c.wait()
    row_pos = lax.axis_index("row")
    col = cols[...]
    owner = div(col, blk)
    far = div(owner, ncol) ^ row_pos
    slot = (far & 1) * (nrow // 2) + div(far, 2)
    table[pl.ds(0, 1), :] = slot * blk + col - owner * blk
    live = lax.broadcasted_iota(jnp.int32, (1, nt), 1) < count[0]
    table[pl.ds(1, 1), :] = jnp.where(live, rows[...] - row_pos * (blk * ncol), blk * ncol)
    for i in range(COPIES):
        copy(i).wait()


def spread(seeded, nrow, ncol, blk, *refs):
    tiles, table_in, refs = refs[0], refs[1], refs[2:]
    fields, refs = refs[:nrow], refs[nrow:]
    outs, refs = refs[:ncol], refs[ncol:]
    total, picks, table, sem = refs
    nt = tiles.shape[0]
    col_pos = lax.axis_index("col")
    load = pltpu.make_async_copy(table_in, table, sem)
    load.start()
    total[...] = jnp.zeros_like(total)
    if seeded:
        for i, f in enumerate(fields):
            for kind in range(2):
                picks[kind, pl.ds(i * blk, blk), :] = f[kind].astype(jnp.float32)
    else:
        for i, f in enumerate(fields):
            picks[pl.ds(i * blk, blk)] = f[...]
    query = lax.broadcasted_iota(jnp.int32, (QC, 128), 0).astype(jnp.float32)
    load.wait()

    def pick(t):
        place = table[0, t]
        if seeded:
            label = picks[0, pl.ds(place, 1), :]
            scale = picks[1, pl.ds(place, 1), :]
            return jnp.where(label == query, scale, 0.0).astype(jnp.bfloat16)
        return picks[place]

    def step(i, carry):
        terms = []
        for u in range(0, UNROLL, 2):
            t = i * UNROLL + u
            pair = lax.dot_general(
                jnp.concatenate([pick(t), pick(t + 1)], 0),
                tiles[pl.ds(t, 2)].reshape(256, 128),
                (((1,), (1,)), ((), ())),
                preferred_element_type=jnp.float32,
            )
            terms += [pair[:QC, :128], pair[QC:, 128:]]
        for u in range(UNROLL):
            total[table[1, i * UNROLL + u]] += terms[u]
        return carry

    lax.fori_loop(0, nt // UNROLL, step, 0)
    for k in range(ncol):
        part = total[pl.ds((col_pos ^ k) * blk, blk)]
        outs[k][...] = part.astype(outs[k].dtype)


def fetch_call(nrow, ncol, blk, tiles, rows, cols, count):
    nt = tiles.shape[0]
    return pl.pallas_call(
        functools.partial(fetch, nrow, ncol, blk),
        out_shape=[VMEM(tiles.shape, tiles.dtype), VMEM((2, nt), jnp.int32)],
        in_specs=[pl.BlockSpec(memory_space=HBM)] * 3 + [pl.BlockSpec(memory_space=SMEM)],
        out_specs=[pl.BlockSpec(memory_space=VMEM)] * 2,
        scratch_shapes=[VMEM((1, nt), jnp.int32)] * 2 + [pltpu.SemaphoreType.DMA((COPIES + 2,))],
        compiler_params=pltpu.CompilerParams(vmem_limit_bytes=16 << 20),
        cost_estimate=pl.CostEstimate(flops=0, bytes_accessed=tiles.size * 2, transcendentals=0),
    )(*(pltpu.with_memory_space_constraint(x, HBM) for x in (tiles, rows.reshape(1, nt), cols.reshape(1, nt))), count)


def spread_call(seeded, nrow, ncol, blk, tiles, table, fields):
    nt = tiles.shape[0]
    slots = nrow * blk
    shape = (blk, QC, 128)
    picks = pltpu.VMEM((2, slots, 128), jnp.float32) if seeded else pltpu.VMEM((slots, QC, 128), jnp.bfloat16)
    return pl.pallas_call(
        functools.partial(spread, seeded, nrow, ncol, blk),
        out_shape=[jax.ShapeDtypeStruct(shape, jnp.float32)]
        + [jax.ShapeDtypeStruct(shape, jnp.bfloat16)] * (ncol - 1),
        in_specs=[pl.BlockSpec(memory_space=VMEM)] * (2 + len(fields)),
        out_specs=[pl.BlockSpec(memory_space=VMEM)] * ncol,
        scratch_shapes=[
            pltpu.VMEM((blk * ncol + 1, QC, 128), jnp.float32),
            picks,
            pltpu.SMEM(table.shape, table.dtype),
            pltpu.SemaphoreType.DMA,
        ],
        compiler_params=pltpu.CompilerParams(vmem_limit_bytes=24 << 20),
        cost_estimate=pl.CostEstimate(
            flops=2 * nt * QC * 128 * 128, bytes_accessed=tiles.size * 2 + slots * QC * 256, transcendentals=0
        ),
    )(*(pltpu.with_memory_space_constraint(x, VMEM) for x in (tiles, table)), *fields)


def local(nrow, ncol, tiles, tile_rows, tile_cols, tile_count, degree, labels):
    blk = labels.shape[0]
    nz = nrow // 2

    def from_row(x, d):
        return lax.ppermute(x, "row", [(i, i ^ d) for i in range(nrow)])

    def from_col(x, k):
        return lax.ppermute(x, "col", [(i, i ^ k) for i in range(ncol)])

    scale = 1.0 / jnp.sqrt(degree.astype(jnp.float32))
    qidx = jnp.arange(QC, dtype=jnp.int32)
    prior = (labels[:, None, :] == qidx[None, :, None]).astype(jnp.float32)
    kind = lax.broadcasted_iota(jnp.int32, (2, 1, 1), 0)
    raw = jnp.where(kind == 0, labels[None], degree[None]).astype(jnp.float32)
    own = jnp.where(kind == 0, raw, 1.0 / jnp.sqrt(raw)).astype(jnp.bfloat16)
    tiles, table = fetch_call(nrow, ncol, blk, tiles, tile_rows, tile_cols, tile_count)
    for step in range(ITERS):
        if step > 0:
            own = (field * scale[:, None, :]).astype(jnp.bfloat16)
        near = [own] + [from_row(own, 2 * m) for m in range(1, nz)]
        if step == 0:
            near[-1], table = lax.optimization_barrier((near[-1], table))
        fields = near + [from_row(x, 1) for x in near]
        outs = spread_call(step == 0, nrow, ncol, blk, tiles, table, fields)
        summed = outs[0]
        for k in range(1, ncol):
            summed = summed + from_col(outs[k], k).astype(jnp.float32)
        field = 0.8 * scale[:, None, :] * summed + 0.2 * prior
    return field


def solution(mesh):
    nrow, ncol = mesh.shape["row"], mesh.shape["col"]
    return jax.shard_map(
        functools.partial(local, nrow, ncol),
        mesh=mesh,
        in_specs=(
            P(("row", "col"), None, None),
            P(("row", "col")),
            P(("row", "col")),
            P(("row", "col")),
            P(("row", "col"), None),
            P(("row", "col"), None),
        ),
        out_specs=P(("row", "col"), None, None),
        check_vma=False,
    )
```

```python
import functools

import jax
import jax.numpy as jnp
from jax import lax
from jax.experimental import pallas as pl
from jax.experimental.pallas import tpu as pltpu
from jax.sharding import PartitionSpec as P

QC = 16
ITERS = 2
COPIES = 8
UNROLL = 64

HBM = pltpu.HBM
VMEM = pltpu.VMEM
SMEM = pltpu.SMEM


def div(value, size):
    if size & (size - 1) == 0:
        return lax.shift_right_logical(value, jnp.full_like(value, size.bit_length() - 1))
    return lax.div(value, jnp.full_like(value, size))


def fetch(nrow, ncol, blk, tiles_hbm, rows_hbm, cols_hbm, count, tiles, table_out, rows, cols, table, sem):
    nt = tiles.shape[0]
    part = nt // COPIES

    def copy(i):
        some = pl.ds(i * part, part)
        return pltpu.make_async_copy(tiles_hbm.at[some], tiles.at[some], sem.at[i])

    tables = [
        pltpu.make_async_copy(source, target, sem.at[COPIES + i])
        for i, (source, target) in enumerate(((rows_hbm, rows), (cols_hbm, cols)))
    ]
    for c in tables:
        c.start()
    for i in range(COPIES):
        copy(i).start()
    for c in tables:
        c.wait()
    row_pos = lax.axis_index("row")
    col = cols[...]
    owner = div(col, blk)
    far = div(owner, ncol) ^ row_pos
    slot = (far & 1) * (nrow // 2) + div(far, 2)
    table[pl.ds(0, 1), :] = slot * blk + col - owner * blk
    live = lax.broadcasted_iota(jnp.int32, (1, nt), 1) < count[0]
    table[pl.ds(1, 1), :] = jnp.where(live, rows[...] - row_pos * (blk * ncol), blk * ncol)
    out = pltpu.make_async_copy(table, table_out, sem.at[COPIES + 2])
    out.start()
    for i in range(COPIES):
        copy(i).wait()
    out.wait()


def spread(seeded, nrow, ncol, blk, *refs):
    tiles, table, refs = refs[0], refs[1], refs[2:]
    nfields = nrow // 2 if seeded else nrow
    fields, refs = refs[:nfields], refs[nfields:]
    outs, refs = refs[:ncol], refs[ncol:]
    total, picks = refs
    nt = tiles.shape[0]
    col_pos = lax.axis_index("col")
    total[...] = jnp.zeros_like(total)
    if seeded:
        for i, f in enumerate(fields):
            for half in range(2):
                for kind in range(2):
                    place = (half * len(fields) + i) * blk
                    picks[kind, pl.ds(place, blk), :] = f[half, kind].astype(jnp.float32)
    else:
        for i, f in enumerate(fields):
            picks[pl.ds(i * blk, blk)] = f[...]
    query = lax.broadcasted_iota(jnp.int32, (QC, 128), 0).astype(jnp.float32)

    def pick(t):
        place = table[0, t]
        if seeded:
            label = picks[0, pl.ds(place, 1), :]
            scale = picks[1, pl.ds(place, 1), :]
            return jnp.where(label == query, scale, 0.0).astype(jnp.bfloat16)
        return picks[place]

    def step(i, carry):
        terms = []
        for u in range(0, UNROLL, 2):
            t = i * UNROLL + u
            pair = lax.dot_general(
                jnp.concatenate([pick(t), pick(t + 1)], 0),
                tiles[pl.ds(t, 2)].reshape(256, 128),
                (((1,), (1,)), ((), ())),
                preferred_element_type=jnp.float32,
            )
            terms += [pair[:QC, :128], pair[QC:, 128:]]
        for u in range(UNROLL):
            total[table[1, i * UNROLL + u]] += terms[u]
        return carry

    lax.fori_loop(0, nt // UNROLL, step, 0)
    for k in range(ncol):
        part = total[pl.ds((col_pos ^ k) * blk, blk)]
        outs[k][...] = part.astype(outs[k].dtype)


def fetch_call(nrow, ncol, blk, tiles, rows, cols, count):
    nt = tiles.shape[0]
    return pl.pallas_call(
        functools.partial(fetch, nrow, ncol, blk),
        out_shape=[VMEM(tiles.shape, tiles.dtype), SMEM((2, nt), jnp.int32)],
        in_specs=[pl.BlockSpec(memory_space=HBM)] * 3 + [pl.BlockSpec(memory_space=SMEM)],
        out_specs=[pl.BlockSpec(memory_space=VMEM), pl.BlockSpec(memory_space=SMEM)],
        scratch_shapes=[VMEM((1, nt), jnp.int32)] * 2 + [VMEM((2, nt), jnp.int32), pltpu.SemaphoreType.DMA((COPIES + 3,))],
        compiler_params=pltpu.CompilerParams(vmem_limit_bytes=16 << 20),
        cost_estimate=pl.CostEstimate(flops=0, bytes_accessed=tiles.size * 2, transcendentals=0),
    )(*(pltpu.with_memory_space_constraint(x, HBM) for x in (tiles, rows.reshape(1, nt), cols.reshape(1, nt))), count)


def spread_call(seeded, nrow, ncol, blk, tiles, table, fields):
    nt = tiles.shape[0]
    slots = nrow * blk
    shape = (blk, QC, 128)
    picks = pltpu.VMEM((2, slots, 128), jnp.float32) if seeded else pltpu.VMEM((slots, QC, 128), jnp.bfloat16)
    return pl.pallas_call(
        functools.partial(spread, seeded, nrow, ncol, blk),
        out_shape=[jax.ShapeDtypeStruct(shape, jnp.float32)]
        + [jax.ShapeDtypeStruct(shape, jnp.bfloat16)] * (ncol - 1),
        in_specs=[pl.BlockSpec(memory_space=VMEM), pl.BlockSpec(memory_space=SMEM)]
        + [pl.BlockSpec(memory_space=VMEM)] * len(fields),
        out_specs=[pl.BlockSpec(memory_space=VMEM)] * ncol,
        scratch_shapes=[
            pltpu.VMEM((blk * ncol + 1, QC, 128), jnp.float32),
            picks,
        ],
        compiler_params=pltpu.CompilerParams(vmem_limit_bytes=24 << 20),
        cost_estimate=pl.CostEstimate(
            flops=2 * nt * QC * 128 * 128, bytes_accessed=tiles.size * 2 + slots * QC * 256, transcendentals=0
        ),
    )(pltpu.with_memory_space_constraint(tiles, VMEM), pltpu.with_memory_space_constraint(table, SMEM), *fields)


def local(nrow, ncol, tiles, tile_rows, tile_cols, tile_count, degree, labels):
    blk = labels.shape[0]
    nz = nrow // 2

    def from_row(x, d):
        return lax.ppermute(x, "row", [(i, i ^ d) for i in range(nrow)])

    def from_col(x, k):
        return lax.ppermute(x, "col", [(i, i ^ k) for i in range(ncol)])

    scale = 1.0 / jnp.sqrt(degree.astype(jnp.float32))
    qidx = jnp.arange(QC, dtype=jnp.int32)
    prior = (labels[:, None, :] == qidx[None, :, None]).astype(jnp.float32)
    kind = lax.broadcasted_iota(jnp.int32, (2, 1, 1), 0)
    raw = jnp.where(kind == 0, labels[None], degree[None]).astype(jnp.float32)
    own = jnp.where(kind == 0, raw, 1.0 / jnp.sqrt(raw)).astype(jnp.bfloat16)
    tiles, table = fetch_call(nrow, ncol, blk, tiles, tile_rows, tile_cols, tile_count)
    for step in range(ITERS):
        if step > 0:
            own = (field * scale[:, None, :]).astype(jnp.bfloat16)
        if step == 0:
            own = lax.optimization_barrier(own)
            both = jnp.stack([own, from_row(own, 1)])
            fields = [both] + [from_row(both, 2 * m) for m in range(1, nz)]
        else:
            near = [own] + [from_row(own, 2 * m) for m in range(1, nz)]
            fields = near + [from_row(x, 1) for x in near]
        outs = spread_call(step == 0, nrow, ncol, blk, tiles, table, fields)
        summed = outs[0]
        for k in range(1, ncol):
            summed = summed + from_col(outs[k], k).astype(jnp.float32)
        field = 0.8 * scale[:, None, :] * summed + 0.2 * prior
    return field


def solution(mesh):
    nrow, ncol = mesh.shape["row"], mesh.shape["col"]
    return jax.shard_map(
        functools.partial(local, nrow, ncol),
        mesh=mesh,
        in_specs=(
            P(("row", "col"), None, None),
            P(("row", "col")),
            P(("row", "col")),
            P(("row", "col")),
            P(("row", "col"), None),
            P(("row", "col"), None),
        ),
        out_specs=P(("row", "col"), None, None),
        check_vma=False,
    )
```

```python
import functools

import jax
import jax.numpy as jnp
from jax import lax
from jax.experimental import pallas as pl
from jax.experimental.pallas import tpu as pltpu
from jax.sharding import PartitionSpec as P

QC = 16
ITERS = 2
COPIES = 8
UNROLL = 32

HBM = pltpu.HBM
VMEM = pltpu.VMEM
SMEM = pltpu.SMEM


def div(value, size):
    if size & (size - 1) == 0:
        return lax.shift_right_logical(value, jnp.full_like(value, size.bit_length() - 1))
    return lax.div(value, jnp.full_like(value, size))


def parts_of(ncol):
    far = max(1, ncol // 4)
    return [(ncol - far, ncol), (1, ncol - far), (0, 1)]


def fetch(nrow, ncol, blk, tiles_hbm, rows_hbm, cols_hbm, count, tiles, table_out, rows, cols, table, sem):
    nt = tiles.shape[0]
    part = nt // COPIES

    def copy(i):
        some = pl.ds(i * part, part)
        return pltpu.make_async_copy(tiles_hbm.at[some], tiles.at[some], sem.at[i])

    tables = [
        pltpu.make_async_copy(source, target, sem.at[COPIES + i])
        for i, (source, target) in enumerate(((rows_hbm, rows), (cols_hbm, cols)))
    ]
    for c in tables:
        c.start()
    for i in range(COPIES):
        copy(i).start()
    for c in tables:
        c.wait()
    row_pos, col_pos = lax.axis_index("row"), lax.axis_index("col")
    col = cols[...]
    owner = div(col, blk)
    far = div(owner, ncol) ^ row_pos
    slot = (far & 1) * (nrow // 2) + div(far, 2)
    place = slot * blk + col - owner * blk
    row = rows[...] - row_pos * (blk * ncol)
    target = div(row, blk)
    slice_ = target ^ col_pos
    row = row - target * blk + slice_ * blk
    parts = parts_of(ncol)
    key = sum((slice_ < low).astype(jnp.int32) for low, _ in parts[:-1])
    lane = lax.broadcasted_iota(jnp.int32, (1, nt), 1)
    key = jnp.where(lane < count[0], key, len(parts)).astype(jnp.float32)
    across = lax.broadcasted_iota(jnp.int32, (nt, nt), 1).astype(jnp.float32)
    down = lax.broadcasted_iota(jnp.int32, (nt, nt), 0).astype(jnp.float32)
    same = across == down

    def stand(x):
        return jnp.sum(jnp.where(same, jnp.broadcast_to(x.astype(jnp.float32), (nt, nt)), 0.0), 1, keepdims=True)

    key_down = stand(key)
    ahead = (key < key_down) | ((key == key_down) & (across < down))
    rank = jnp.sum(jnp.where(ahead, 1.0, 0.0), 1, keepdims=True)
    chosen = rank == across

    def pull(x):
        return jnp.sum(jnp.where(chosen, x, 0.0), 0, keepdims=True).astype(jnp.int32)

    table[...] = jnp.zeros_like(table)
    table[pl.ds(0, 1), pl.ds(0, nt)] = pull(stand(place))
    table[pl.ds(1, 1), pl.ds(0, nt)] = pull(stand(row))
    table[pl.ds(2, 1), pl.ds(0, nt)] = pull(down)
    table[pl.ds(3, 1), pl.ds(0, nt)] = jnp.sum(
        jnp.where(key_down < across, 1.0, 0.0), 0, keepdims=True
    ).astype(jnp.int32)
    out = pltpu.make_async_copy(table, table_out, sem.at[COPIES + 2])
    out.start()
    for i in range(COPIES):
        copy(i).wait()
    out.wait()


def spread(seeded, first, index, part, nrow, ncol, blk, *refs):
    low, high = part
    tiles, table, refs = refs[0], refs[1], refs[2:]
    if first:
        nfields = nrow // 2 if seeded else nrow
        fields, refs = refs[:nfields], refs[nfields:]
    else:
        picks, refs = refs[0], refs[1:]
    outs, refs = refs[: high - low], refs[high - low :]
    if first:
        picks, refs = refs[0], refs[1:]
    (total,) = refs
    total[...] = jnp.zeros_like(total)
    if first and seeded:
        for i, f in enumerate(fields):
            for half in range(2):
                for kind in range(2):
                    place = (half * len(fields) + i) * blk
                    picks[kind, pl.ds(place, blk), :] = f[half, kind].astype(jnp.float32)
    elif first:
        for i, f in enumerate(fields):
            picks[pl.ds(i * blk, blk)] = f[...]
    query = lax.broadcasted_iota(jnp.int32, (QC, 128), 0).astype(jnp.float32)
    begin, end = table[3, index], table[3, index + 1]

    def pick(t):
        place = table[0, t]
        if seeded:
            label = picks[0, pl.ds(place, 1), :]
            scale = picks[1, pl.ds(place, 1), :]
            return jnp.where(label == query, scale, 0.0).astype(jnp.bfloat16)
        return picks[place]

    def step(i, carry):
        base = begin + i * UNROLL
        terms = []
        for u in range(0, UNROLL, 2):
            t = base + u
            pair = lax.dot_general(
                jnp.concatenate([pick(t), pick(t + 1)], 0),
                jnp.concatenate([tiles[table[2, t]], tiles[table[2, t + 1]]], 0),
                (((1,), (1,)), ((), ())),
                preferred_element_type=jnp.float32,
            )
            terms += [pair[:QC, :128], pair[QC:, 128:]]
        for u in range(UNROLL):
            t = base + u
            total[jnp.where(t < end, table[1, t] - low * blk, (high - low) * blk)] += terms[u]
        return carry

    lax.fori_loop(0, lax.div(end - begin + (UNROLL - 1), UNROLL), step, 0)
    for k in range(high - low):
        outs[k][...] = total[pl.ds(k * blk, blk)].astype(outs[k].dtype)


def fetch_call(nrow, ncol, blk, tiles, rows, cols, count):
    nt = tiles.shape[0]
    wide = (4, nt + 128)
    return pl.pallas_call(
        functools.partial(fetch, nrow, ncol, blk),
        out_shape=[VMEM(tiles.shape, tiles.dtype), SMEM(wide, jnp.int32)],
        in_specs=[pl.BlockSpec(memory_space=HBM)] * 3 + [pl.BlockSpec(memory_space=SMEM)],
        out_specs=[pl.BlockSpec(memory_space=VMEM), pl.BlockSpec(memory_space=SMEM)],
        scratch_shapes=[VMEM((1, nt), jnp.int32)] * 2
        + [VMEM(wide, jnp.int32), pltpu.SemaphoreType.DMA((COPIES + 3,))],
        compiler_params=pltpu.CompilerParams(vmem_limit_bytes=16 << 20),
        cost_estimate=pl.CostEstimate(flops=0, bytes_accessed=tiles.size * 2, transcendentals=0),
    )(*(pltpu.with_memory_space_constraint(x, HBM) for x in (tiles, rows.reshape(1, nt), cols.reshape(1, nt))), count)


def spread_calls(seeded, nrow, ncol, blk, tiles, table, fields):
    nt = tiles.shape[0]
    slots = nrow * blk
    shape = (blk, QC, 128)
    picks = VMEM((2, slots, 128), jnp.float32) if seeded else VMEM((slots, QC, 128), jnp.bfloat16)
    slices = [None] * ncol
    arrays = fields
    for index, (low, high) in enumerate(parts_of(ncol)):
        first = index == 0
        share = max(1, (high - low) * nt // ncol)
        results = pl.pallas_call(
            functools.partial(spread, seeded, first, index, (low, high), nrow, ncol, blk),
            out_shape=[
                jax.ShapeDtypeStruct(shape, jnp.float32 if k == 0 else jnp.bfloat16) for k in range(low, high)
            ]
            + [picks] * first,
            in_specs=[pl.BlockSpec(memory_space=VMEM), pl.BlockSpec(memory_space=SMEM)]
            + [pl.BlockSpec(memory_space=VMEM)] * len(arrays),
            out_specs=[pl.BlockSpec(memory_space=VMEM)] * (high - low + first),
            scratch_shapes=[VMEM(((high - low) * blk + 1, QC, 128), jnp.float32)],
            compiler_params=pltpu.CompilerParams(vmem_limit_bytes=24 << 20),
            cost_estimate=pl.CostEstimate(
                flops=2 * share * QC * 128 * 128, bytes_accessed=share * 128 * 256, transcendentals=0
            ),
        )(
            pltpu.with_memory_space_constraint(tiles, VMEM),
            pltpu.with_memory_space_constraint(table, SMEM),
            *arrays,
        )
        slices[low:high] = results[: high - low]
        if first:
            arrays = [pltpu.with_memory_space_constraint(results[-1], VMEM)]
    return slices


def local(nrow, ncol, tiles, tile_rows, tile_cols, tile_count, degree, labels):
    blk = labels.shape[0]
    nz = nrow // 2

    def from_row(x, d):
        return lax.ppermute(x, "row", [(i, i ^ d) for i in range(nrow)])

    def from_col(x, k):
        return lax.ppermute(x, "col", [(i, i ^ k) for i in range(ncol)])

    scale = 1.0 / jnp.sqrt(degree.astype(jnp.float32))
    qidx = jnp.arange(QC, dtype=jnp.int32)
    prior = (labels[:, None, :] == qidx[None, :, None]).astype(jnp.float32)
    kind = lax.broadcasted_iota(jnp.int32, (2, 1, 1), 0)
    raw = jnp.where(kind == 0, labels[None], degree[None]).astype(jnp.float32)
    own = jnp.where(kind == 0, raw, 1.0 / jnp.sqrt(raw)).astype(jnp.bfloat16)
    tiles, table = fetch_call(nrow, ncol, blk, tiles, tile_rows, tile_cols, tile_count)
    for step in range(ITERS):
        if step > 0:
            own = (field * scale[:, None, :]).astype(jnp.bfloat16)
        if step == 0:
            own = lax.optimization_barrier(own)
            both = jnp.stack([own, from_row(own, 1)])
            fields = [both] + [from_row(both, 2 * m) for m in range(1, nz)]
        else:
            near = [own] + [from_row(own, 2 * m) for m in range(1, nz)]
            fields = near + [from_row(x, 1) for x in near]
        outs = spread_calls(step == 0, nrow, ncol, blk, tiles, table, fields)
        summed = outs[0]
        for k in range(1, ncol):
            summed = summed + from_col(outs[k], k).astype(jnp.float32)
        field = 0.8 * scale[:, None, :] * summed + 0.2 * prior
    return field


def solution(mesh):
    nrow, ncol = mesh.shape["row"], mesh.shape["col"]
    return jax.shard_map(
        functools.partial(local, nrow, ncol),
        mesh=mesh,
        in_specs=(
            P(("row", "col"), None, None),
            P(("row", "col")),
            P(("row", "col")),
            P(("row", "col")),
            P(("row", "col"), None),
            P(("row", "col"), None),
        ),
        out_specs=P(("row", "col"), None, None),
        check_vma=False,
    )
```

```python
import functools

import jax
import jax.numpy as jnp
from jax import lax
from jax.experimental import pallas as pl
from jax.experimental.pallas import tpu as pltpu
from jax.sharding import PartitionSpec as P

QC = 16
ITERS = 2
COPIES = 8
UNROLL = 32

HBM = pltpu.HBM
VMEM = pltpu.VMEM
SMEM = pltpu.SMEM


def div(value, size):
    if size & (size - 1) == 0:
        return lax.shift_right_logical(value, jnp.full_like(value, size.bit_length() - 1))
    return lax.div(value, jnp.full_like(value, size))


def parts_of(ncol):
    far = max(1, ncol // 4)
    return [(ncol - far, ncol), (1, ncol - far), (0, 1)]


def fetch(nrow, ncol, blk, tiles_hbm, rows_hbm, cols_hbm, count, tiles, table_out, rows, cols, table, sem):
    nt = tiles.shape[0]
    part = nt // COPIES

    def copy(i):
        some = pl.ds(i * part, part)
        return pltpu.make_async_copy(tiles_hbm.at[some], tiles.at[some], sem.at[i])

    tables = [
        pltpu.make_async_copy(source, target, sem.at[COPIES + i])
        for i, (source, target) in enumerate(((rows_hbm, rows), (cols_hbm, cols)))
    ]
    for c in tables:
        c.start()
    for i in range(COPIES):
        copy(i).start()
    for c in tables:
        c.wait()
    row_pos, col_pos = lax.axis_index("row"), lax.axis_index("col")
    col = cols[...]
    owner = div(col, blk)
    far = div(owner, ncol) ^ row_pos
    slot = (far & 1) * (nrow // 2) + div(far, 2)
    place = slot * blk + col - owner * blk
    row = rows[...] - row_pos * (blk * ncol)
    target = div(row, blk)
    slice_ = target ^ col_pos
    row = row - target * blk + slice_ * blk
    parts = parts_of(ncol)
    key = sum((slice_ < low).astype(jnp.int32) for low, _ in parts[:-1])
    lane = lax.broadcasted_iota(jnp.int32, (1, nt), 1)
    key = jnp.where(lane < count[0], key, len(parts)).astype(jnp.float32)
    across = lax.broadcasted_iota(jnp.int32, (nt, nt), 1).astype(jnp.float32)
    down = lax.broadcasted_iota(jnp.int32, (nt, nt), 0).astype(jnp.float32)
    same = across == down

    def stand(x):
        return jnp.sum(jnp.where(same, jnp.broadcast_to(x.astype(jnp.float32), (nt, nt)), 0.0), 1, keepdims=True)

    key_down = stand(key)
    ahead = (key < key_down) | ((key == key_down) & (across < down))
    rank = jnp.sum(jnp.where(ahead, 1.0, 0.0), 1, keepdims=True)
    chosen = rank == across

    def pull(x):
        return jnp.sum(jnp.where(chosen, x, 0.0), 0, keepdims=True).astype(jnp.int32)

    table[...] = jnp.zeros_like(table)
    table[pl.ds(0, 1), pl.ds(0, nt)] = pull(stand(place))
    table[pl.ds(1, 1), pl.ds(0, nt)] = pull(stand(row))
    table[pl.ds(2, 1), pl.ds(0, nt)] = pull(down)
    table[pl.ds(3, 1), pl.ds(0, nt)] = jnp.sum(
        jnp.where(key_down < across, 1.0, 0.0), 0, keepdims=True
    ).astype(jnp.int32)
    out = pltpu.make_async_copy(table, table_out, sem.at[COPIES + 2])
    out.start()
    for i in range(COPIES):
        copy(i).wait()
    out.wait()


def spread(seeded, first, index, part, nrow, ncol, blk, *refs):
    low, high = part
    tiles, table, refs = refs[0], refs[1], refs[2:]
    if first:
        nfields = nrow // 2 if seeded else nrow
        fields, refs = refs[:nfields], refs[nfields:]
    else:
        picks, refs = refs[0], refs[1:]
    outs, refs = refs[: high - low], refs[high - low :]
    if first:
        picks, refs = refs[0], refs[1:]
    (total,) = refs
    total[...] = jnp.zeros_like(total)
    if first and seeded:
        for i, f in enumerate(fields):
            for half in range(2):
                for kind in range(2):
                    place = (half * len(fields) + i) * blk
                    picks[kind, pl.ds(place, blk), :] = f[half, kind].astype(jnp.float32)
    elif first:
        near = slots_of(nrow, lax.axis_index("row"))
        for i, f in enumerate(fields):
            slot = near[i % (nrow // 2)] + i // (nrow // 2) * (nrow // 2)
            picks[pl.ds(slot * blk, blk)] = f[...]
    query = lax.broadcasted_iota(jnp.int32, (QC, 128), 0).astype(jnp.float32)
    begin, end = table[3, index], table[3, index + 1]

    def pick(t):
        place = table[0, t]
        if seeded:
            label = picks[0, pl.ds(place, 1), :]
            scale = picks[1, pl.ds(place, 1), :]
            return jnp.where(label == query, scale, 0.0).astype(jnp.bfloat16)
        return picks[place]

    def step(i, carry):
        base = begin + i * UNROLL
        terms = []
        for u in range(0, UNROLL, 2):
            t = base + u
            pair = lax.dot_general(
                jnp.concatenate([pick(t), pick(t + 1)], 0),
                jnp.concatenate([tiles[table[2, t]], tiles[table[2, t + 1]]], 0),
                (((1,), (1,)), ((), ())),
                preferred_element_type=jnp.float32,
            )
            terms += [pair[:QC, :128], pair[QC:, 128:]]
        for u in range(UNROLL):
            t = base + u
            total[jnp.where(t < end, table[1, t] - low * blk, (high - low) * blk)] += terms[u]
        return carry

    lax.fori_loop(0, lax.div(end - begin + (UNROLL - 1), UNROLL), step, 0)
    for k in range(high - low):
        outs[k][...] = total[pl.ds(k * blk, blk)].astype(outs[k].dtype)


def fetch_call(nrow, ncol, blk, tiles, rows, cols, count):
    nt = tiles.shape[0]
    wide = (4, nt + 128)
    return pl.pallas_call(
        functools.partial(fetch, nrow, ncol, blk),
        out_shape=[VMEM(tiles.shape, tiles.dtype), SMEM(wide, jnp.int32)],
        in_specs=[pl.BlockSpec(memory_space=HBM)] * 3 + [pl.BlockSpec(memory_space=SMEM)],
        out_specs=[pl.BlockSpec(memory_space=VMEM), pl.BlockSpec(memory_space=SMEM)],
        scratch_shapes=[VMEM((1, nt), jnp.int32)] * 2
        + [VMEM(wide, jnp.int32), pltpu.SemaphoreType.DMA((COPIES + 3,))],
        compiler_params=pltpu.CompilerParams(vmem_limit_bytes=16 << 20),
        cost_estimate=pl.CostEstimate(flops=0, bytes_accessed=tiles.size * 2, transcendentals=0),
    )(*(pltpu.with_memory_space_constraint(x, HBM) for x in (tiles, rows.reshape(1, nt), cols.reshape(1, nt))), count)


def spread_calls(seeded, nrow, ncol, blk, tiles, table, fields):
    nt = tiles.shape[0]
    slots = nrow * blk
    shape = (blk, QC, 128)
    picks = VMEM((2, slots, 128), jnp.float32) if seeded else VMEM((slots, QC, 128), jnp.bfloat16)
    slices = [None] * ncol
    arrays = fields
    for index, (low, high) in enumerate(parts_of(ncol)):
        first = index == 0
        share = max(1, (high - low) * nt // ncol)
        results = pl.pallas_call(
            functools.partial(spread, seeded, first, index, (low, high), nrow, ncol, blk),
            out_shape=[
                jax.ShapeDtypeStruct(shape, jnp.float32 if k == 0 else jnp.bfloat16) for k in range(low, high)
            ]
            + [picks] * first,
            in_specs=[pl.BlockSpec(memory_space=VMEM), pl.BlockSpec(memory_space=SMEM)]
            + [pl.BlockSpec(memory_space=VMEM)] * len(arrays),
            out_specs=[pl.BlockSpec(memory_space=VMEM)] * (high - low + first),
            scratch_shapes=[VMEM(((high - low) * blk + 1, QC, 128), jnp.float32)],
            compiler_params=pltpu.CompilerParams(vmem_limit_bytes=24 << 20),
            cost_estimate=pl.CostEstimate(
                flops=2 * share * QC * 128 * 128, bytes_accessed=share * 128 * 256, transcendentals=0
            ),
        )(
            pltpu.with_memory_space_constraint(tiles, VMEM),
            pltpu.with_memory_space_constraint(table, SMEM),
            *arrays,
        )
        slices[low:high] = results[: high - low]
        if first:
            arrays = [pltpu.with_memory_space_constraint(results[-1], VMEM)]
    return slices


def gather_far(own, nrow):
    nz = nrow // 2
    if nz != 4:
        return [lax.ppermute(own, "row", [(i, i ^ (2 * m)) for i in range(nrow)]) for m in range(1, nz)], lax.ppermute(own, "row", [(i, i ^ 1) for i in range(nrow)])
    ring = [(0, 2), (2, 3), (3, 1), (1, 0)]
    ahead = [(2 * a + k, 2 * b + k) for a, b in ring for k in range(2)]
    back = [(b, a) for a, b in ahead]
    one = lax.ppermute(own, "row", ahead)
    partner = lax.ppermute(own, "row", [(i, i ^ 1) for i in range(nrow)])
    later, partner = lax.optimization_barrier((own, partner))
    other = lax.ppermute(later, "row", back)
    return [one, other, lax.ppermute(one, "row", ahead)], partner


def slots_of(nrow, row_pos):
    nz = nrow // 2
    if nz != 4:
        return list(range(nz))
    z = div(row_pos, 2)
    inner = (z ^ div(z, 2)) & 1
    return [0, 1 + inner, 2 - inner, 3]


def local(nrow, ncol, tiles, tile_rows, tile_cols, tile_count, degree, labels):
    blk = labels.shape[0]
    nz = nrow // 2

    def from_row(x, d):
        return lax.ppermute(x, "row", [(i, i ^ d) for i in range(nrow)])

    def from_col(x, k):
        return lax.ppermute(x, "col", [(i, i ^ k) for i in range(ncol)])

    scale = 1.0 / jnp.sqrt(degree.astype(jnp.float32))
    qidx = jnp.arange(QC, dtype=jnp.int32)
    prior = (labels[:, None, :] == qidx[None, :, None]).astype(jnp.float32)
    kind = lax.broadcasted_iota(jnp.int32, (2, 1, 1), 0)
    raw = jnp.where(kind == 0, labels[None], degree[None]).astype(jnp.float32)
    own = jnp.where(kind == 0, raw, 1.0 / jnp.sqrt(raw)).astype(jnp.bfloat16)
    tiles, table = fetch_call(nrow, ncol, blk, tiles, tile_rows, tile_cols, tile_count)
    for step in range(ITERS):
        if step > 0:
            own = (field * scale[:, None, :]).astype(jnp.bfloat16)
        if step == 0:
            own = lax.optimization_barrier(own)
            both = jnp.stack([own, from_row(own, 1)])
            fields = [both] + [from_row(both, 2 * m) for m in range(1, nz)]
        else:
            far, partner = gather_far(own, nrow)
            fields = [own] + far + [partner] + [from_row(x, 1) for x in far]
        outs = spread_calls(step == 0, nrow, ncol, blk, tiles, table, fields)
        summed = outs[0]
        for k in range(1, ncol):
            summed = summed + from_col(outs[k], k).astype(jnp.float32)
        field = 0.8 * scale[:, None, :] * summed + 0.2 * prior
    return field


def solution(mesh):
    nrow, ncol = mesh.shape["row"], mesh.shape["col"]
    return jax.shard_map(
        functools.partial(local, nrow, ncol),
        mesh=mesh,
        in_specs=(
            P(("row", "col"), None, None),
            P(("row", "col")),
            P(("row", "col")),
            P(("row", "col")),
            P(("row", "col"), None),
            P(("row", "col"), None),
        ),
        out_specs=P(("row", "col"), None, None),
        check_vma=False,
    )
```

```python
import functools

import jax
import jax.numpy as jnp
from jax import lax
from jax.experimental import pallas as pl
from jax.experimental.pallas import tpu as pltpu
from jax.sharding import PartitionSpec as P

QC = 16
ITERS = 2
COPIES = 8
UNROLL = 32

HBM = pltpu.HBM
VMEM = pltpu.VMEM
SMEM = pltpu.SMEM


def div(value, size):
    if size & (size - 1) == 0:
        return lax.shift_right_logical(value, jnp.full_like(value, size.bit_length() - 1))
    return lax.div(value, jnp.full_like(value, size))


def parts_of(ncol):
    far = max(1, ncol // 4)
    return [(ncol - far, ncol), (1, ncol - far), (0, 1)]


def fetch(nrow, ncol, blk, tiles_hbm, rows_hbm, cols_hbm, count, tiles, table_out, rows, cols, table, sem):
    nt = tiles.shape[0]
    part = nt // COPIES

    def copy(i):
        some = pl.ds(i * part, part)
        return pltpu.make_async_copy(tiles_hbm.at[some], tiles.at[some], sem.at[i])

    tables = [
        pltpu.make_async_copy(source, target, sem.at[COPIES + i])
        for i, (source, target) in enumerate(((rows_hbm, rows), (cols_hbm, cols)))
    ]
    for c in tables:
        c.start()
    for i in range(COPIES):
        copy(i).start()
    for c in tables:
        c.wait()
    row_pos, col_pos = lax.axis_index("row"), lax.axis_index("col")
    col = cols[...]
    owner = div(col, blk)
    far = div(owner, ncol) ^ row_pos
    slot = (far & 1) * (nrow // 2) + div(far, 2)
    place = slot * blk + col - owner * blk
    row = rows[...] - row_pos * (blk * ncol)
    target = div(row, blk)
    slice_ = target ^ col_pos
    row = row - target * blk + slice_ * blk
    parts = parts_of(ncol)
    key = sum((slice_ < low).astype(jnp.int32) for low, _ in parts[:-1])
    lane = lax.broadcasted_iota(jnp.int32, (1, nt), 1)
    key = jnp.where(lane < count[...], key, len(parts)).astype(jnp.float32)
    across = lax.broadcasted_iota(jnp.int32, (nt, nt), 1).astype(jnp.float32)
    down = lax.broadcasted_iota(jnp.int32, (nt, nt), 0).astype(jnp.float32)
    same = across == down

    def stand(x):
        return jnp.sum(jnp.where(same, jnp.broadcast_to(x.astype(jnp.float32), (nt, nt)), 0.0), 1, keepdims=True)

    key_down = stand(key)
    ahead = (key < key_down) | ((key == key_down) & (across < down))
    rank = jnp.sum(jnp.where(ahead, 1.0, 0.0), 1, keepdims=True)
    chosen = rank == across

    def pull(x):
        return jnp.sum(jnp.where(chosen, x, 0.0), 0, keepdims=True).astype(jnp.int32)

    table[...] = jnp.zeros_like(table)
    table[pl.ds(0, 1), pl.ds(0, nt)] = pull(stand(place))
    table[pl.ds(1, 1), pl.ds(0, nt)] = pull(stand(row))
    table[pl.ds(2, 1), pl.ds(0, nt)] = pull(down)
    table[pl.ds(3, 1), pl.ds(0, nt)] = jnp.sum(
        jnp.where(key_down < across, 1.0, 0.0), 0, keepdims=True
    ).astype(jnp.int32)
    out = pltpu.make_async_copy(table, table_out, sem.at[COPIES + 2])
    out.start()
    for i in range(COPIES):
        copy(i).wait()
    out.wait()


def spread(seeded, first, index, part, nrow, ncol, blk, *refs):
    low, high = part
    tiles, table, refs = refs[0], refs[1], refs[2:]
    if first:
        nfields = nrow // 2 if seeded else nrow
        fields, refs = refs[:nfields], refs[nfields:]
    else:
        picks, refs = refs[0], refs[1:]
    outs, refs = refs[: high - low], refs[high - low :]
    if first:
        picks, refs = refs[0], refs[1:]
    (total,) = refs
    total[...] = jnp.zeros_like(total)
    if first and seeded:
        for i, f in enumerate(fields):
            for half in range(2):
                for kind in range(2):
                    place = (half * len(fields) + i) * blk
                    picks[kind, pl.ds(place, blk), :] = f[half, kind].astype(jnp.float32)
    elif first:
        near = slots_of(nrow, lax.axis_index("row"))
        for i, f in enumerate(fields):
            slot = near[i % (nrow // 2)] + i // (nrow // 2) * (nrow // 2)
            picks[pl.ds(slot * blk, blk)] = f[...]
    query = lax.broadcasted_iota(jnp.int32, (QC, 128), 0).astype(jnp.float32)
    begin, end = table[3, index], table[3, index + 1]

    def pick(t):
        place = table[0, t]
        if seeded:
            label = picks[0, pl.ds(place, 1), :]
            scale = picks[1, pl.ds(place, 1), :]
            return jnp.where(label == query, scale, 0.0).astype(jnp.bfloat16)
        return picks[place]

    def step(i, carry):
        base = begin + i * UNROLL
        terms = []
        for u in range(0, UNROLL, 2):
            t = base + u
            pair = lax.dot_general(
                jnp.concatenate([pick(t), pick(t + 1)], 0),
                jnp.concatenate([tiles[table[2, t]], tiles[table[2, t + 1]]], 0),
                (((1,), (1,)), ((), ())),
                preferred_element_type=jnp.float32,
            )
            terms += [pair[:QC, :128], pair[QC:, 128:]]
        for u in range(UNROLL):
            t = base + u
            total[jnp.where(t < end, table[1, t] - low * blk, (high - low) * blk)] += terms[u]
        return carry

    lax.fori_loop(0, lax.div(end - begin + (UNROLL - 1), UNROLL), step, 0)
    for k in range(high - low):
        outs[k][...] = total[pl.ds(k * blk, blk)].astype(outs[k].dtype)


def fetch_call(nrow, ncol, blk, tiles, rows, cols, count):
    nt = tiles.shape[0]
    wide = (4, nt + 128)
    return pl.pallas_call(
        functools.partial(fetch, nrow, ncol, blk),
        out_shape=[VMEM(tiles.shape, tiles.dtype), SMEM(wide, jnp.int32)],
        in_specs=[pl.BlockSpec(memory_space=HBM)] * 3 + [pl.BlockSpec(memory_space=VMEM)],
        out_specs=[pl.BlockSpec(memory_space=VMEM), pl.BlockSpec(memory_space=SMEM)],
        scratch_shapes=[VMEM((1, nt), jnp.int32)] * 2
        + [VMEM(wide, jnp.int32), pltpu.SemaphoreType.DMA((COPIES + 3,))],
        compiler_params=pltpu.CompilerParams(vmem_limit_bytes=16 << 20),
        cost_estimate=pl.CostEstimate(flops=0, bytes_accessed=tiles.size * 2, transcendentals=0),
    )(*(pltpu.with_memory_space_constraint(x, HBM) for x in (tiles, rows.reshape(1, nt), cols.reshape(1, nt))), count)


def spread_calls(seeded, nrow, ncol, blk, tiles, table, fields):
    nt = tiles.shape[0]
    slots = nrow * blk
    shape = (blk, QC, 128)
    picks = VMEM((2, slots, 128), jnp.float32) if seeded else VMEM((slots, QC, 128), jnp.bfloat16)
    slices = [None] * ncol
    arrays = fields
    for index, (low, high) in enumerate(parts_of(ncol)):
        first = index == 0
        share = max(1, (high - low) * nt // ncol)
        results = pl.pallas_call(
            functools.partial(spread, seeded, first, index, (low, high), nrow, ncol, blk),
            out_shape=[
                jax.ShapeDtypeStruct(shape, jnp.float32 if k == 0 else jnp.bfloat16) for k in range(low, high)
            ]
            + [picks] * first,
            in_specs=[pl.BlockSpec(memory_space=VMEM), pl.BlockSpec(memory_space=SMEM)]
            + [pl.BlockSpec(memory_space=VMEM)] * len(arrays),
            out_specs=[pl.BlockSpec(memory_space=VMEM)] * (high - low + first),
            scratch_shapes=[VMEM(((high - low) * blk + 1, QC, 128), jnp.float32)],
            compiler_params=pltpu.CompilerParams(vmem_limit_bytes=24 << 20),
            cost_estimate=pl.CostEstimate(
                flops=2 * share * QC * 128 * 128, bytes_accessed=share * 128 * 256, transcendentals=0
            ),
        )(
            pltpu.with_memory_space_constraint(tiles, VMEM),
            pltpu.with_memory_space_constraint(table, SMEM),
            *arrays,
        )
        slices[low:high] = results[: high - low]
        if first:
            arrays = [pltpu.with_memory_space_constraint(results[-1], VMEM)]
    return slices


def gather_far(own, nrow):
    nz = nrow // 2
    across = [(i, i ^ 1) for i in range(nrow)]
    if nz != 4:
        far = [lax.ppermute(own, "row", [(i, i ^ (2 * m)) for i in range(nrow)]) for m in range(1, nz)]
        return far, lax.ppermute(own, "row", across)
    ring = [(0, 2), (2, 3), (3, 1), (1, 0)]
    ahead = [(2 * a + k, 2 * b + k) for a, b in ring for k in range(2)]
    back = [(b, a) for a, b in ahead]
    one = lax.ppermute(own, "row", ahead)
    partner = lax.ppermute(own, "row", across)
    later, partner = lax.optimization_barrier((own, partner))
    other = lax.ppermute(later, "row", back)
    return [one, other, lax.ppermute(one, "row", ahead)], partner


def slots_of(nrow, row_pos):
    nz = nrow // 2
    if nz != 4:
        return list(range(nz))
    z = div(row_pos, 2)
    inner = (z ^ div(z, 2)) & 1
    return [0, 1 + inner, 2 - inner, 3]


def local(nrow, ncol, tiles, tile_rows, tile_cols, tile_count, degree, labels):
    blk = labels.shape[0]
    nz = nrow // 2

    def from_row(x, d):
        return lax.ppermute(x, "row", [(i, i ^ d) for i in range(nrow)])

    def from_col(x, k):
        return lax.ppermute(x, "col", [(i, i ^ k) for i in range(ncol)])

    scale = 1.0 / jnp.sqrt(degree.astype(jnp.float32))
    qidx = jnp.arange(QC, dtype=jnp.int32)
    prior = (labels[:, None, :] == qidx[None, :, None]).astype(jnp.float32)
    kind = lax.broadcasted_iota(jnp.int32, (2, 1, 1), 0)
    raw = jnp.where(kind == 0, labels[None], degree[None]).astype(jnp.float32)
    own = jnp.where(kind == 0, raw, 1.0 / jnp.sqrt(raw)).astype(jnp.bfloat16)
    own = lax.optimization_barrier(own)
    other, count = lax.optimization_barrier((from_row(own, 1), jnp.broadcast_to(tile_count, (1, tiles.shape[0]))))
    both = jnp.stack([own, other])
    tiles, table = fetch_call(nrow, ncol, blk, tiles, tile_rows, tile_cols, count)
    for step in range(ITERS):
        if step > 0:
            own = (field * scale[:, None, :]).astype(jnp.bfloat16)
        if step == 0:
            fields = [both] + [from_row(both, 2 * m) for m in range(1, nz)]
        else:
            far, partner = gather_far(own, nrow)
            fields = [own] + far + [partner] + [from_row(x, 1) for x in far]
        outs = spread_calls(step == 0, nrow, ncol, blk, tiles, table, fields)
        summed = outs[0]
        for k in range(1, ncol):
            summed = summed + from_col(outs[k], k).astype(jnp.float32)
        field = 0.8 * scale[:, None, :] * summed + 0.2 * prior
    return field


def solution(mesh):
    nrow, ncol = mesh.shape["row"], mesh.shape["col"]
    return jax.shard_map(
        functools.partial(local, nrow, ncol),
        mesh=mesh,
        in_specs=(
            P(("row", "col"), None, None),
            P(("row", "col")),
            P(("row", "col")),
            P(("row", "col")),
            P(("row", "col"), None),
            P(("row", "col"), None),
        ),
        out_specs=P(("row", "col"), None, None),
        check_vma=False,
    )
```

```python
import functools

import jax
import jax.numpy as jnp
from jax import lax
from jax.experimental import pallas as pl
from jax.experimental.pallas import tpu as pltpu
from jax.sharding import PartitionSpec as P

QC = 16
ITERS = 2
COPIES = 8
UNROLL = 32

HBM = pltpu.HBM
VMEM = pltpu.VMEM
SMEM = pltpu.SMEM


def div(value, size):
    if size & (size - 1) == 0:
        return lax.shift_right_logical(value, jnp.full_like(value, size.bit_length() - 1))
    return lax.div(value, jnp.full_like(value, size))


def parts_of(ncol):
    far = max(1, ncol // 4)
    return [(ncol - far, ncol), (1, ncol - far), (0, 1)]


def fetch(nrow, ncol, blk, tiles_hbm, rows_hbm, cols_hbm, count, tiles, table_out, rows, cols, table, sem):
    nt = tiles.shape[0]
    part = nt // COPIES

    def copy(i):
        some = pl.ds(i * part, part)
        return pltpu.make_async_copy(tiles_hbm.at[some], tiles.at[some], sem.at[i])

    tables = [
        pltpu.make_async_copy(source, target, sem.at[COPIES + i])
        for i, (source, target) in enumerate(((rows_hbm, rows), (cols_hbm, cols)))
    ]
    for c in tables:
        c.start()
    for i in range(COPIES):
        copy(i).start()
    for c in tables:
        c.wait()
    row_pos, col_pos = lax.axis_index("row"), lax.axis_index("col")
    col = cols[...]
    owner = div(col, blk)
    far = div(owner, ncol) ^ row_pos
    slot = (far & 1) * (nrow // 2) + div(far, 2)
    place = slot * blk + col - owner * blk
    row = rows[...] - row_pos * (blk * ncol)
    target = div(row, blk)
    slice_ = target ^ col_pos
    row = row - target * blk + slice_ * blk
    parts = parts_of(ncol)
    key = sum((slice_ < low).astype(jnp.int32) for low, _ in parts[:-1])
    lane = lax.broadcasted_iota(jnp.int32, (1, nt), 1)
    key = jnp.where(lane < count[...], key, len(parts)).astype(jnp.float32)
    across = lax.broadcasted_iota(jnp.int32, (nt, nt), 1).astype(jnp.float32)
    down = lax.broadcasted_iota(jnp.int32, (nt, nt), 0).astype(jnp.float32)
    same = across == down

    def stand(x):
        return jnp.sum(jnp.where(same, jnp.broadcast_to(x.astype(jnp.float32), (nt, nt)), 0.0), 1, keepdims=True)

    key_down = stand(key)
    ahead = (key < key_down) | ((key == key_down) & (across < down))
    rank = jnp.sum(jnp.where(ahead, 1.0, 0.0), 1, keepdims=True)
    chosen = rank == across

    def pull(x):
        return jnp.sum(jnp.where(chosen, x, 0.0), 0, keepdims=True).astype(jnp.int32)

    table[...] = jnp.zeros_like(table)
    table[pl.ds(0, 1), pl.ds(0, nt)] = pull(stand(place))
    table[pl.ds(1, 1), pl.ds(0, nt)] = pull(stand(row))
    table[pl.ds(2, 1), pl.ds(0, nt)] = pull(down)
    table[pl.ds(3, 1), pl.ds(0, nt)] = jnp.sum(
        jnp.where(key_down < across, 1.0, 0.0), 0, keepdims=True
    ).astype(jnp.int32)
    out = pltpu.make_async_copy(table, table_out, sem.at[COPIES + 2])
    out.start()
    for i in range(COPIES):
        copy(i).wait()
    out.wait()


def spread(seeded, first, index, part, nrow, ncol, blk, *refs):
    low, high = part
    tiles, table, refs = refs[0], refs[1], refs[2:]
    if first:
        nfields = nrow // 2 if seeded else nrow
        fields, refs = refs[:nfields], refs[nfields:]
    else:
        picks, refs = refs[0], refs[1:]
    outs, refs = refs[: high - low], refs[high - low :]
    if first:
        picks, refs = refs[0], refs[1:]
    (total,) = refs
    total[...] = jnp.zeros_like(total)
    if first and seeded:
        for i, f in enumerate(fields):
            for half in range(2):
                for kind in range(2):
                    place = (half * len(fields) + i) * blk
                    picks[kind, pl.ds(place, blk), :] = f[half, kind].astype(jnp.float32)
    elif first:
        near = slots_of(nrow, lax.axis_index("row"))
        for i, f in enumerate(fields):
            slot = near[i % (nrow // 2)] + i // (nrow // 2) * (nrow // 2)
            picks[pl.ds(slot * blk, blk)] = f[...]
    query = lax.broadcasted_iota(jnp.int32, (QC, 128), 0).astype(jnp.float32)
    begin, end = table[3, index], table[3, index + 1]

    def pick(t):
        place = table[0, t]
        if seeded:
            label = picks[0, pl.ds(place, 1), :]
            scale = picks[1, pl.ds(place, 1), :]
            return jnp.where(label == query, scale, 0.0).astype(jnp.bfloat16)
        return picks[place]

    unroll = (24, 32, 16)[index]

    def step(i, carry):
        base = begin + i * unroll
        terms = []
        for u in range(0, unroll, 2):
            t = base + u
            pair = lax.dot_general(
                jnp.concatenate([pick(t), pick(t + 1)], 0),
                jnp.concatenate([tiles[table[2, t]], tiles[table[2, t + 1]]], 0),
                (((1,), (1,)), ((), ())),
                preferred_element_type=jnp.float32,
            )
            terms += [pair[:QC, :128], pair[QC:, 128:]]
        for u in range(unroll):
            t = base + u
            total[jnp.where(t < end, table[1, t] - low * blk, (high - low) * blk)] += terms[u]
        return carry

    lax.fori_loop(0, lax.div(end - begin + (unroll - 1), unroll), step, 0)
    for k in range(high - low):
        outs[k][...] = total[pl.ds(k * blk, blk)].astype(outs[k].dtype)


def fetch_call(nrow, ncol, blk, tiles, rows, cols, count):
    nt = tiles.shape[0]
    wide = (4, nt + 128)
    return pl.pallas_call(
        functools.partial(fetch, nrow, ncol, blk),
        out_shape=[VMEM(tiles.shape, tiles.dtype), SMEM(wide, jnp.int32)],
        in_specs=[pl.BlockSpec(memory_space=HBM)] * 3 + [pl.BlockSpec(memory_space=VMEM)],
        out_specs=[pl.BlockSpec(memory_space=VMEM), pl.BlockSpec(memory_space=SMEM)],
        scratch_shapes=[VMEM((1, nt), jnp.int32)] * 2
        + [VMEM(wide, jnp.int32), pltpu.SemaphoreType.DMA((COPIES + 3,))],
        compiler_params=pltpu.CompilerParams(vmem_limit_bytes=16 << 20),
        cost_estimate=pl.CostEstimate(flops=0, bytes_accessed=tiles.size * 2, transcendentals=0),
    )(*(pltpu.with_memory_space_constraint(x, HBM) for x in (tiles, rows.reshape(1, nt), cols.reshape(1, nt))), count)


def spread_calls(seeded, nrow, ncol, blk, tiles, table, fields):
    nt = tiles.shape[0]
    slots = nrow * blk
    shape = (blk, QC, 128)
    picks = VMEM((2, slots, 128), jnp.float32) if seeded else VMEM((slots, QC, 128), jnp.bfloat16)
    slices = [None] * ncol
    arrays = fields
    for index, (low, high) in enumerate(parts_of(ncol)):
        first = index == 0
        share = max(1, (high - low) * nt // ncol)
        results = pl.pallas_call(
            functools.partial(spread, seeded, first, index, (low, high), nrow, ncol, blk),
            out_shape=[
                jax.ShapeDtypeStruct(shape, jnp.float32 if k == 0 else jnp.bfloat16) for k in range(low, high)
            ]
            + [picks] * first,
            in_specs=[pl.BlockSpec(memory_space=VMEM), pl.BlockSpec(memory_space=SMEM)]
            + [pl.BlockSpec(memory_space=VMEM)] * len(arrays),
            out_specs=[pl.BlockSpec(memory_space=VMEM)] * (high - low + first),
            scratch_shapes=[VMEM(((high - low) * blk + 1, QC, 128), jnp.float32)],
            compiler_params=pltpu.CompilerParams(vmem_limit_bytes=24 << 20),
            cost_estimate=pl.CostEstimate(
                flops=2 * share * QC * 128 * 128, bytes_accessed=share * 128 * 256, transcendentals=0
            ),
        )(
            pltpu.with_memory_space_constraint(tiles, VMEM),
            pltpu.with_memory_space_constraint(table, SMEM),
            *arrays,
        )
        slices[low:high] = results[: high - low]
        if first:
            arrays = [pltpu.with_memory_space_constraint(results[-1], VMEM)]
    return slices


def finish(ncol, *refs):
    own, came, scale, labels, out, field, sem = refs[0], refs[1:ncol], *refs[ncol:]
    blk = own.shape[0]
    part = blk // 4
    query = lax.broadcasted_iota(jnp.int32, (QC, 128), 0)
    copies = []
    for i in range(4):
        for b in range(i * part, (i + 1) * part):
            summed = own[b]
            for x in came:
                summed = summed + x[b].astype(jnp.float32)
            prior = jnp.where(labels[pl.ds(b, 1), :] == query, 0.2, 0.0)
            field[b] = 0.8 * scale[pl.ds(b, 1), :] * summed + prior
        some = pl.ds(i * part, part)
        copies.append(pltpu.make_async_copy(field.at[some], out.at[some], sem.at[i]))
        copies[-1].start()
    for c in copies:
        c.wait()


def finish_call(own, came, scale, labels):
    return pl.pallas_call(
        functools.partial(finish, 1 + len(came)),
        out_shape=jax.ShapeDtypeStruct(own.shape, jnp.float32),
        in_specs=[pl.BlockSpec(memory_space=VMEM)] * (3 + len(came)),
        out_specs=pl.BlockSpec(memory_space=pl.ANY),
        scratch_shapes=[VMEM(own.shape, jnp.float32), pltpu.SemaphoreType.DMA((4,))],
        compiler_params=pltpu.CompilerParams(vmem_limit_bytes=16 << 20),
        cost_estimate=pl.CostEstimate(flops=8 * own.size, bytes_accessed=12 * own.size, transcendentals=0),
    )(own, *came, scale, labels)


def gather_far(own, nrow):
    nz = nrow // 2
    if nz != 4:
        return [lax.ppermute(own, "row", [(i, i ^ (2 * m)) for i in range(nrow)]) for m in range(1, nz)], lax.ppermute(own, "row", [(i, i ^ 1) for i in range(nrow)])
    ring = [(0, 2), (2, 3), (3, 1), (1, 0)]
    ahead = [(2 * a + k, 2 * b + k) for a, b in ring for k in range(2)]
    back = [(b, a) for a, b in ahead]
    one = lax.ppermute(own, "row", ahead)
    partner = lax.ppermute(own, "row", [(i, i ^ 1) for i in range(nrow)])
    later, partner = lax.optimization_barrier((own, partner))
    other = lax.ppermute(later, "row", back)
    return [one, other, lax.ppermute(one, "row", ahead)], partner


def slots_of(nrow, row_pos):
    nz = nrow // 2
    if nz != 4:
        return list(range(nz))
    z = div(row_pos, 2)
    inner = (z ^ div(z, 2)) & 1
    return [0, 1 + inner, 2 - inner, 3]


def local(nrow, ncol, tiles, tile_rows, tile_cols, tile_count, degree, labels):
    blk = labels.shape[0]
    nz = nrow // 2

    def from_row(x, d):
        return lax.ppermute(x, "row", [(i, i ^ d) for i in range(nrow)])

    def from_col(x, k):
        return lax.ppermute(x, "col", [(i, i ^ k) for i in range(ncol)])

    scale = 1.0 / jnp.sqrt(degree.astype(jnp.float32))
    qidx = jnp.arange(QC, dtype=jnp.int32)
    prior = (labels[:, None, :] == qidx[None, :, None]).astype(jnp.float32)
    kind = lax.broadcasted_iota(jnp.int32, (2, 1, 1), 0)
    raw = jnp.where(kind == 0, labels[None], degree[None]).astype(jnp.float32)
    own = jnp.where(kind == 0, raw, 1.0 / jnp.sqrt(raw)).astype(jnp.bfloat16)
    own = lax.optimization_barrier(own)
    other, count = lax.optimization_barrier((from_row(own, 1), jnp.broadcast_to(tile_count, (1, tiles.shape[0]))))
    both = jnp.stack([own, other])
    tiles, table = fetch_call(nrow, ncol, blk, tiles, tile_rows, tile_cols, count)
    for step in range(ITERS):
        if step > 0:
            own = (field * scale[:, None, :]).astype(jnp.bfloat16)
        if step == 0:
            fields = [both] + [from_row(both, 2 * m) for m in range(1, nz)]
        else:
            far, partner = gather_far(own, nrow)
            fields = [own] + far + [partner] + [from_row(x, 1) for x in far]
        outs = spread_calls(step == 0, nrow, ncol, blk, tiles, table, fields)
        came = [from_col(outs[k], k) for k in range(1, ncol)]
        if step == ITERS - 1:
            return finish_call(outs[0], came, scale, labels)
        summed = outs[0]
        for x in came:
            summed = summed + x.astype(jnp.float32)
        field = 0.8 * scale[:, None, :] * summed + 0.2 * prior
    return field


def solution(mesh):
    nrow, ncol = mesh.shape["row"], mesh.shape["col"]
    return jax.shard_map(
        functools.partial(local, nrow, ncol),
        mesh=mesh,
        in_specs=(
            P(("row", "col"), None, None),
            P(("row", "col")),
            P(("row", "col")),
            P(("row", "col")),
            P(("row", "col"), None),
            P(("row", "col"), None),
        ),
        out_specs=P(("row", "col"), None, None),
        check_vma=False,
    )
```
